32 devices in a mesh: groups: 2 (over y), tiles: 8 (over z, core), ens: 2 (over x), lev: 1.
Axes of the slice: x: 2, y: 2, z: 4, core: 2. Of those that a mesh axis runs over, the one named last changes fastest.
Arguments:
- inputs: bfloat16 [2, 1, 16, 3, 32, 32, 128], P('ens', 'lev', ('groups', 'tiles')), parts along dimension 2, may hold values from -6 to 6
- slot_rows: int32 [16, 3], P('groups'), parts along dimension 0, may hold values from -1 to 3, as said below
- cell_mask: int32 [1, 16, 3, 32, 32], P('lev', ('groups', 'tiles')), parts along dimension 1, may hold values 0 or 1
- target: bfloat16 [1, 16, 3, 4, 32, 32], P('lev', ('groups', 'tiles')), parts along dimension 1, may hold values from -24 to 24
- dw_kernel: float32 [7, 7, 128], replicated, may hold values from -0.875 to 0.875
- dw_bias: float32 [128], replicated, may hold values from -3 to 3
- ln_gain: float32 [128], replicated, may hold values from 0.1 to 1.9
- ln_bias: float32 [128], replicated, may hold values from -3 to 3
- w_in: bfloat16 [128, 256], replicated, may hold values from -0.5 to 0.5
- b_in: float32 [256], replicated, may hold values from -3 to 3
- w_out: bfloat16 [256, 128], replicated, may hold values from -0.375 to 0.375
- b_out: float32 [128], replicated, may hold values from -3 to 3
- layer_scale: float32 [128], replicated, may hold values from 0.3 to 1.5
- w_head: float32 [128, 4], replicated, may hold values from -2 to 2
Outputs:
- grad_x: bfloat16 [2, 1, 16, 3, 32, 32, 128], P('ens', 'lev', ('groups', 'tiles')), parts along dimension 2
- crps: bfloat16 [1, 16, 3, 32, 32], P('lev', ('groups', 'tiles'), None, 'ens'), parts along dimension 1
The draws below stay inside these ranges and needn't reach their ends.
There are 2 independent parts, one for each index of `groups`. The reference program is written for one: setup_inputs(seed, part) draws one part's arguments, and reference() takes and returns one part's arrays. A program takes and returns all parts, laid end to end along the dimension named above; an argument that names none is the same for every part. Nothing has to cross between parts.
Inputs may be any that keep to these rules, and one draw needn't show every extreme that they name: `slot_rows`: each row c lists the tile rows of the ocean tiles of tile column c in increasing order, each at most once, followed by -1 in the empty slots. Tile columns c and c + 4 hold 4 ocean tiles together; every column holds 1 to 3, and some column holds exactly 3.
All inputs are finite; a program needn't handle non-finite values. No bound on the sum of `cell_mask` on one device may be relied on, other than what follows from the above.
Results may differ from the reference program's by a relative error of at most 0.012.
Values may be sent and summed in bfloat16 or wider, within the bound.
A program may use at most 64 MiB of HBM per device.

```python
import math
import jax
import jax.numpy as jnp
from jax import lax

C = 128
HID = 256
NV = 4
KERNEL = 7
TILE = 32
PAIR_TILES = 4
SLOTS = 3
COLS = 8
MEMBERS = 2
LEVELS = 1


def draw_slot_rows(key, part):
    half_cols = COLS // 2
    key_count, key_pick, key_side, key_rows = jax.random.split(key, 4)
    counts_low = jax.random.randint(key_count, (half_cols,), 1, PAIR_TILES)
    chosen = jax.random.randint(key_pick, (), 0, half_cols)
    side = jax.random.randint(key_side, (), 0, 2)
    forced = jnp.where(side == 0, PAIR_TILES - 1, 1)
    counts_low = jnp.where(jnp.arange(half_cols) == chosen, forced, counts_low)
    counts = jnp.concatenate([counts_low, PAIR_TILES - counts_low])

    def shuffled(row_key):
        return jax.random.permutation(row_key, PAIR_TILES)
    order = jax.vmap(shuffled)(jax.random.split(key_rows, COLS))
    position = jnp.argsort(order, axis=1)
    selected = position < counts[:, None]
    row_ids = jnp.arange(PAIR_TILES, dtype=jnp.int32)[None, :]
    keyed = jnp.where(selected, row_ids, PAIR_TILES + row_ids)
    ordered = jnp.sort(keyed, axis=1)[:, :PAIR_TILES - 1]
    return jnp.where(ordered < PAIR_TILES, ordered, -1).astype(jnp.int32)


def touch_ends(entries, stream_key, low, largest):
    longest = entries.shape.index(max(entries.shape))
    spots = []
    for shift in (0, 1):
        where = [jax.random.randint(jax.random.fold_in(stream_key, axis), (), 0, length) for axis, length in enumerate(entries.shape)]
        where[longest] = (where[longest] + shift) % entries.shape[longest]
        spots.append(tuple(where))
    return entries.at[spots[0]].set(low).at[spots[1]].set(largest)


def block_levels(own_key, extent, cuts, least, top_value):
    def one(axis_at, shards_of):
        heights = jax.random.uniform(jax.random.fold_in(jax.random.fold_in(own_key, 6), axis_at), (shards_of,), jnp.float32, least / len(cuts), top_value / len(cuts))
        return jnp.repeat(jnp.exp(heights), extent[axis_at] // shards_of).reshape((-1,) + (1,) * (len(extent) - axis_at - 1))

    gain = one(*cuts[0])
    for cut in cuts[1:]:
        gain = gain * one(*cut)
    return gain


def gaussian(own_key, extent, scale, limit, cuts=(), kind=jnp.bfloat16):
    loudness = block_levels(own_key, extent, cuts, -0.22, 0.18) if cuts else 1.0
    array = jax.random.normal(own_key, extent, jnp.float32) * scale * loudness
    return jnp.minimum(jnp.maximum(array, -limit), limit).astype(kind)


def setup_inputs(seed: int = 0, part: int = 0) -> dict:
    arg_keys = jax.random.split(jax.random.key(seed), 15)
    own_keys = jax.random.split(jax.random.fold_in(arg_keys[14], part), 15)
    inputs = gaussian(own_keys[0], (MEMBERS, LEVELS, COLS, SLOTS, TILE, TILE, C), 1.0, 6.0, ((0, 2), (2, 8)))
    slot_rows = draw_slot_rows(jax.random.fold_in(jax.random.fold_in(arg_keys[14], part), 71), part)
    cell_mask = touch_ends((jax.random.randint(own_keys[2], (LEVELS, COLS, SLOTS, TILE, TILE), 0, 8) < 7).astype(jnp.int32), jax.random.fold_in(own_keys[2], 1), 0, 1)
    target = gaussian(own_keys[3], (LEVELS, COLS, SLOTS, NV, TILE, TILE), 4.0, 24.0, ((1, 8),))
    dw_kernel = gaussian(arg_keys[4], (KERNEL, KERNEL, C), (KERNEL * KERNEL) ** -0.5, 0.875, (), jnp.float32)
    dw_bias = gaussian(arg_keys[5], (C,), 0.5, 3.0, (), jnp.float32)
    ln_gain = jnp.clip(1.0 + 0.18 * jax.random.normal(arg_keys[6], (C,), jnp.float32), 0.1, 1.9)
    ln_bias = gaussian(arg_keys[7], (C,), 0.5, 3.0, (), jnp.float32)
    w_in = gaussian(arg_keys[8], (C, HID), C ** -0.5, 0.5)
    b_in = gaussian(arg_keys[9], (HID,), 0.5, 3.0, (), jnp.float32)
    w_out = gaussian(arg_keys[10], (HID, C), HID ** -0.5, 0.375)
    b_out = gaussian(arg_keys[11], (C,), 0.5, 3.0, (), jnp.float32)
    layer_scale = jnp.clip(jnp.exp(jax.random.uniform(arg_keys[12], (C,), jnp.float32, math.log(0.3), math.log(1.5))), 0.3, 1.5)
    w_head = gaussian(arg_keys[13], (C, NV), 0.35, 2.0, (), jnp.float32)
    return {"inputs": inputs, "slot_rows": slot_rows, "cell_mask": cell_mask, "target": target, "dw_kernel": dw_kernel, "dw_bias": dw_bias, "ln_gain": ln_gain, "ln_bias": ln_bias, "w_in": w_in, "b_in": b_in, "w_out": w_out, "b_out": b_out, "layer_scale": layer_scale, "w_head": w_head}


softness = 0.0625
epsilon = 1e-06
highest = lax.Precision.HIGHEST

def soft_abs(value):
    return jnp.sqrt(value * value + softness)

def soft_sign(value):
    return value / jnp.sqrt(value * value + softness)

def gelu_slope(value):
    cumulative = 0.5 * (1.0 + lax.erf(value * 0.7071067811865476))
    return cumulative + value * jnp.exp(-0.5 * value * value) * 0.3989422804014327

def place_grid(tiles, onehot):
    placed = jnp.einsum('csr,csabk->rcabk', onehot, tiles, precision=highest)
    grid_rows = placed.shape[0]
    columns = placed.shape[1]
    tile = placed.shape[2]
    width = placed.shape[4]
    return placed.transpose(0, 2, 1, 3, 4).reshape(grid_rows * tile, columns * tile, width)

def take_grid(grid, onehot, tile):
    grid_rows = onehot.shape[2]
    columns = onehot.shape[0]
    width = grid.shape[2]
    blocks = grid.reshape(grid_rows, tile, columns, tile, width).transpose(0, 2, 1, 3, 4)
    return jnp.einsum('csr,rcabk->csabk', onehot, blocks, precision=highest)

def stencil_grid(grid, weights):
    size = weights.shape[0]
    rim = size // 2
    padded = jnp.pad(grid, ((rim, rim), (0, 0), (0, 0)))
    padded = jnp.concatenate([padded[:, padded.shape[1] - rim:], padded, padded[:, :rim]], axis=1)
    height = grid.shape[0]
    breadth = grid.shape[1]
    total = jnp.zeros(grid.shape, jnp.float32)
    for row_off in range(size):
        for col_off in range(size):
            total = total + weights[row_off, col_off] * padded[row_off:row_off + height, col_off:col_off + breadth]
    return total

def reference(inputs, slot_rows, cell_mask, target, dw_kernel, dw_bias, ln_gain, ln_bias, w_in, b_in, w_out, b_out, layer_scale, w_head):
    members = inputs.shape[0]
    levels = inputs.shape[1]
    columns = inputs.shape[2]
    slots = inputs.shape[3]
    tile = inputs.shape[4]
    width = inputs.shape[6]
    live = (slot_rows >= 0).astype(jnp.float32)
    onehot = (slot_rows[:, :, None] == jnp.arange(PAIR_TILES, dtype=jnp.int32)[None, None, :]).astype(jnp.float32)
    weight_mask = cell_mask.astype(jnp.float32) * live[None, :, :, None, None]
    flipped = dw_kernel[::-1, ::-1]

    def forward(tiles, mask):
        masked_x = tiles.astype(jnp.float32) * mask[..., None]
        conv_out = take_grid(stencil_grid(place_grid(masked_x, onehot), dw_kernel), onehot, tile) + dw_bias
        mean_z = lax.optimization_barrier(jnp.mean(conv_out, axis=-1, keepdims=True))
        centered = conv_out - mean_z
        inv_std = lax.rsqrt(lax.optimization_barrier(jnp.mean(centered * centered, axis=-1, keepdims=True)) + epsilon)
        normed = centered * inv_std
        features = (normed * ln_gain + ln_bias).astype(jnp.bfloat16)
        pre = jnp.dot(features.reshape(-1, width), w_in, preferred_element_type=jnp.float32) + b_in
        act = jax.nn.gelu(pre, approximate=False).astype(jnp.bfloat16)
        branch = jnp.dot(act, w_out, preferred_element_type=jnp.float32) + b_out
        pred = jnp.dot(masked_x.reshape(-1, width), w_head, precision=highest) + jnp.dot(layer_scale * branch, w_head, precision=highest)
        pred = pred.reshape(columns, slots, tile, tile, NV).transpose(0, 1, 4, 2, 3)
        return (pred, inv_std, normed, pre)
    flat_x = inputs.reshape((members * levels,) + inputs.shape[2:])
    flat_mask = jnp.broadcast_to(weight_mask[None], (members,) + weight_mask.shape).reshape((members * levels,) + weight_mask.shape[1:])

    def forward_pred(pair):
        return forward(pair[0], pair[1])[0]
    preds = lax.map(forward_pred, (flat_x, flat_mask)).reshape((members, levels) + (columns, slots, NV, tile, tile))
    observed = target.astype(jnp.float32)
    mask_var = weight_mask[:, :, :, None]
    skill = jnp.zeros(observed.shape, jnp.float32)
    spread = jnp.zeros(observed.shape, jnp.float32)
    for first in range(members):
        skill = skill + soft_abs(preds[first] - observed)
        for second in range(members):
            spread = spread + soft_abs(preds[first] - preds[second])
    skill = skill / members
    spread = spread / (2 * members * members)
    crps = (weight_mask * lax.optimization_barrier(jnp.sum(skill - spread, axis=3))).astype(jnp.bfloat16)
    grads = []
    for first in range(members):
        pair_sum = jnp.zeros(observed.shape, jnp.float32)
        for second in range(members):
            pair_sum = pair_sum + soft_sign(preds[first] - preds[second])
        grads.append((mask_var * (soft_sign(preds[first] - observed) / members - pair_sum / (members * members))).astype(jnp.bfloat16))
    grad_pred = jnp.stack(grads).reshape((members * levels,) + observed.shape[1:])

    def backward(triple):
        tiles, mask, grad_one = triple
        pred, inv_std, normed, pre = forward(tiles, mask)
        grad_rows = jnp.dot(grad_one.astype(jnp.float32).transpose(0, 1, 3, 4, 2).reshape(-1, NV), w_head.T, precision=highest)
        scaled = (layer_scale * grad_rows).astype(jnp.bfloat16)
        grad_act = jnp.dot(scaled, w_out.T, preferred_element_type=jnp.float32)
        grad_pre = (grad_act * gelu_slope(pre)).astype(jnp.bfloat16)
        grad_feat = jnp.dot(grad_pre, w_in.T, preferred_element_type=jnp.float32).astype(jnp.bfloat16)
        gated = grad_feat.astype(jnp.float32).reshape(normed.shape) * ln_gain
        grad_z = (inv_std * (gated - lax.optimization_barrier(jnp.mean(gated, axis=-1, keepdims=True)) - normed * lax.optimization_barrier(jnp.mean(gated * normed, axis=-1, keepdims=True)))).astype(jnp.bfloat16)
        through = take_grid(stencil_grid(place_grid(grad_z.astype(jnp.float32), onehot), flipped), onehot, tile)
        return (mask[..., None] * (grad_rows.reshape(normed.shape) + through)).astype(jnp.bfloat16)
    grad_x = lax.map(backward, (flat_x, flat_mask, grad_pred)).reshape(inputs.shape)
    return (grad_x, crps)
```

```python
import functools

import jax
import jax.numpy as jnp
from jax import lax
from jax.experimental import pallas as pl
from jax.experimental.pallas import tpu as pltpu
from jax.sharding import PartitionSpec as P

softness = 0.0625
epsilon = 1e-06
MESH = pl.DeviceIdType.MESH
f32 = jnp.float32
bf16 = jnp.bfloat16
LEFT = 8
NT = (((1,), (1,)), ((), ()))
TN = (((0,), (0,)), ((), ()))


def soft_abs(value):
    return jnp.sqrt(value * value + softness)


def soft_sign(value):
    return value * lax.rsqrt(value * value + softness)


def kernel(
    members,
    columns,
    rows_ref,
    x_ref,
    m8_ref,
    t8_ref,
    dw_ref,
    dwb_ref,
    gain_ref,
    lnb_ref,
    win_ref,
    bin_ref,
    wout_ref,
    bout_ref,
    ls_ref,
    wh8_ref,
    out_ref,
    crps_ref,
    pad,
    lhs,
    band,
    acc,
    normed,
    invs,
    grows,
    mcol,
    xm,
    feat,
    pre,
    act,
    slope,
    ex,
    hx,
    eg,
    hg,
    pmine,
    pall,
    sx,
    rx,
    sg,
    rg,
    sp,
    rp,
    *,
    slots,
    tile,
    size,
):
    rim = size // 2
    half = tile // 2
    width = x_ref.shape[-1]
    nrow = half * tile
    hidden = win_ref.shape[1]
    pairs = (tile + 2 * rim) // 2
    depth = (size + 1) // 2
    me = lax.axis_index("tiles")
    mine = lax.axis_index("ens")
    west = lax.rem(me + columns - 1, columns)
    east = lax.rem(me + 1, columns)

    barrier = pltpu.get_barrier_semaphore()
    pl.semaphore_signal(barrier, inc=1, device_id={"tiles": west}, device_id_type=MESH)
    pl.semaphore_signal(barrier, inc=1, device_id={"tiles": east}, device_id_type=MESH)
    for p in range(1, members):
        pl.semaphore_signal(
            barrier, inc=1, device_id={"ens": lax.rem(mine + p, members)}, device_id_type=MESH
        )

    sub8 = lax.broadcasted_iota(jnp.int32, (8, 1), 0)
    zero_strip = jnp.zeros((size // 2, tile, width), bf16)
    for side in range(2):
        hx[side, slots] = zero_strip
        hg[side, slots] = zero_strip

    def mask_slot(s, carry):
        m8 = m8_ref[s]
        for b in range(2):
            pick = jnp.broadcast_to((sub8 == 4 * b).astype(bf16), (8, width))
            col = lax.dot_general(m8, pick, TN, preferred_element_type=f32)
            mcol[s, b] = col
            xv = x_ref[s, :, b].astype(f32).reshape(nrow, width) * col
            xm[s, b] = xv.astype(bf16)
            x3 = xv.reshape(half, tile, width)
            for r in range(half):
                pad[s, rim + 2 * r + b, LEFT : LEFT + tile, :] = x3[r]
        return carry

    def strips(s, dst):
        for c in range(rim):
            dst[0, s, c] = pad[s, rim : rim + tile, LEFT + tile - rim + c, :].astype(bf16)
            dst[1, s, c] = pad[s, rim : rim + tile, LEFT + c, :].astype(bf16)

    lax.fori_loop(0, slots, mask_slot, 0)
    for s in range(slots):
        strips(s, ex)

    pl.semaphore_wait(barrier, 2 + members - 1)

    def edge_copy(src, dst, send, recv, side):
        return pltpu.make_async_remote_copy(
            src_ref=src,
            dst_ref=dst,
            send_sem=send,
            recv_sem=recv,
            device_id={"tiles": east if side == 0 else west},
            device_id_type=MESH,
        )

    x_copies = [
        edge_copy(ex.at[side], hx.at[side, pl.ds(0, slots)], sx.at[side], rx.at[side], side)
        for side in range(2)
    ]
    for copy in x_copies:
        copy.start()

    eye = lax.broadcasted_iota(jnp.int32, (width, width), 0) == lax.broadcasted_iota(
        jnp.int32, (width, width), 1
    )
    zero_block = jnp.zeros((width, width), bf16)

    def build_band(j, carry):
        for o in range(2 * depth):
            for b in range(2):
                i = o - b
                if 0 <= i < size:
                    row = dw_ref[j, pl.ds(i, 1), :]
                    block = jnp.where(eye, jnp.broadcast_to(row, (width, width)), 0.0).astype(bf16)
                else:
                    block = zero_block
                band[j, o * width : (o + 1) * width, b * width : (b + 1) * width] = block
        return carry

    lax.fori_loop(0, size, build_band, 0)

    wh8 = wh8_ref[...]
    scaled_head = wh8 * ls_ref[...]
    through_head = lax.dot_general(
        scaled_head, wout_ref[...].astype(f32), NT, precision=lax.Precision.HIGHEST,
        preferred_element_type=f32,
    )
    bias_head = jnp.sum(scaled_head * bout_ref[...], axis=1, keepdims=True)
    both = jnp.concatenate([wh8, through_head], axis=1)
    both_hi = both.astype(bf16)
    both_lo = (both - both_hi.astype(f32)).astype(bf16)
    both_hl = jnp.concatenate([both_hi.astype(f32), both_lo.astype(f32)], axis=0).astype(bf16)
    sub16 = lax.broadcasted_iota(jnp.int32, (16, 1), 0)

    own = [rows_ref[me, s] for s in range(slots)]
    wrow = [rows_ref[west, s] for s in range(slots)]
    erow = [rows_ref[east, s] for s in range(slots)]

    def find(source, wanted):
        place = jnp.int32(slots)
        for t in range(slots):
            place = jnp.where((source[t] >= 0) & (source[t] == wanted), jnp.int32(t), place)
        return place

    def vertical():
        edge = jnp.zeros((rim, tile, width), f32)
        for s in range(slots):
            if s > 0:
                flag = ((own[s] >= 0) & (own[s - 1] == own[s] - 1)).astype(f32)
                pad[s, 0:rim, LEFT : LEFT + tile, :] = (
                    pad[s - 1, tile : tile + rim, LEFT : LEFT + tile, :] * flag
                )
            else:
                pad[s, 0:rim, LEFT : LEFT + tile, :] = edge
            if s < slots - 1:
                flag = ((own[s + 1] >= 0) & (own[s + 1] == own[s] + 1)).astype(f32)
                pad[s, tile + rim : tile + 2 * rim, LEFT : LEFT + tile, :] = (
                    pad[s + 1, rim : 2 * rim, LEFT : LEFT + tile, :] * flag
                )
            else:
                pad[s, tile + rim : tile + 2 * rim, LEFT : LEFT + tile, :] = edge

    def lateral(buf):
        for s in range(slots):
            for side, source in ((0, wrow), (1, erow)):
                up = find(source, own[s] - 1)
                level = find(source, own[s])
                down = find(source, own[s] + 1)
                for c in range(rim):
                    at = LEFT - rim + c if side == 0 else LEFT + tile + c
                    pad[s, rim : rim + tile, at, :] = buf[side, level, c].astype(f32)
                    pad[s, 0:rim, at, :] = buf[side, up, c].astype(f32)[tile - rim :]
                    pad[s, tile + rim : tile + 2 * rim, at, :] = buf[side, down, c].astype(f32)[
                        :rim
                    ]

    def conv(s, flip):
        def gather(m, carry):
            for a in range(2):
                lane = (1 - a if flip else a) * width
                for j in range(size):
                    lhs[j, m, :, lane : lane + width] = pad[
                        s, 2 * m + a, LEFT - rim + j : LEFT - rim + j + tile, :
                    ].astype(bf16)
            return carry

        lax.fori_loop(0, pairs, gather, 0)
        total = None
        for j in range(size):
            parts = [
                lhs[j, (depth - 1 - d if flip else d) : (depth - 1 - d if flip else d) + half]
                .reshape(nrow, 2 * width)
                for d in range(depth)
            ]
            part = jnp.dot(
                jnp.concatenate(parts, axis=1),
                band[size - 1 - j if flip else j],
                preferred_element_type=f32,
            )
            if j == 0:
                acc[...] = part
            else:
                acc[...] += part

    vertical()
    for copy in x_copies:
        copy.wait()
    lateral(hx)

    chunk = 64
    nchunk = nrow // chunk

    def pred_copy(s, p):
        return pltpu.make_async_remote_copy(
            src_ref=pmine.at[s],
            dst_ref=pall.at[p - 1, s],
            send_sem=sp.at[p - 1, s],
            recv_sem=rp.at[p - 1, s],
            device_id={"ens": lax.rem(mine + p, members)},
            device_id_type=MESH,
        )

    def forward(s, carry):
        conv(s, False)
        for b in range(2):

            def norm(q, carry):
                at = pl.ds(pl.multiple_of(q * chunk, chunk), chunk)
                z = acc[at, b * width : (b + 1) * width] + dwb_ref[...]
                mean = jnp.mean(z, axis=1, keepdims=True)
                z = z - mean
                inv = lax.rsqrt(jnp.mean(z * z, axis=1, keepdims=True) + epsilon)
                z = z * inv
                normed[s, b, at, :] = z
                invs[s, b, at, :] = jnp.broadcast_to(inv, (chunk, width))
                feat[b, at, :] = (z * gain_ref[...] + lnb_ref[...]).astype(bf16)
                return carry

            lax.fori_loop(0, nchunk, norm, 0, unroll=2)
        res = []
        for b in range(2):
            pre[...] = jnp.dot(feat[b], win_ref[...], preferred_element_type=f32)

            def gelu(q, carry):
                at = pl.ds(pl.multiple_of(q * chunk, chunk), chunk)
                v = pre[at, :] + bin_ref[...]
                cum = 0.5 * (1.0 + lax.erf(v * 0.7071067811865476))
                act[at, :] = (v * cum).astype(bf16)
                slope[s, b, at, :] = cum + v * jnp.exp(-0.5 * v * v) * 0.3989422804014327
                return carry

            lax.fori_loop(0, nchunk, gelu, 0, unroll=2)
            r16 = lax.dot_general(
                both_hl,
                jnp.concatenate([xm[s, b], act[...]], axis=1),
                NT,
                preferred_element_type=f32,
            )
            res.append(r16[:8] + r16[8:])
        pmine[s] = jnp.where(sub8 < 4, res[0], res[1]) + bias_head
        for p in range(1, members):
            pred_copy(s, p).start()
        return carry

    lax.fori_loop(0, slots, forward, 0)

    def gz_copy(s, side):
        return edge_copy(eg.at[side, s], hg.at[side, s], sg.at[side, s], rg.at[side, s], side)

    def backward(s, carry):
        for p in range(1, members):
            pred_copy(s, p).wait()
        every = [pmine[s]] + [pall[p - 1, s] for p in range(1, members)]
        goal = t8_ref[s].astype(f32)
        mask = m8_ref[s].astype(f32)
        skill = soft_abs(every[0] - goal)
        spread = jnp.zeros_like(skill)
        pull = jnp.zeros_like(skill)
        for p in range(1, members):
            skill = skill + soft_abs(every[p] - goal)
            pull = pull + soft_sign(every[0] - every[p])
            for other in range(p):
                spread = spread + soft_abs(every[p] - every[other])
        diagonal = members * softness**0.5
        score = mask * (
            skill / members - (2.0 * spread + diagonal) / (2 * members * members)
        )
        crps_ref[s] = jnp.concatenate(
            [
                jnp.sum(score[:4], axis=0, keepdims=True),
                jnp.sum(score[4:], axis=0, keepdims=True),
            ],
            axis=0,
        )
        gp = mask * (soft_sign(every[0] - goal) / members - pull / (members * members))
        gp = gp.astype(bf16).astype(f32)
        gp16 = jnp.concatenate([gp, gp], axis=0).astype(bf16)
        for b in range(2):
            rows = (lax.rem(sub16, 8) // 4) == b
            wb = jnp.where(rows, both_hl.astype(f32), 0.0).astype(bf16)
            big = lax.dot_general(gp16, wb, TN, preferred_element_type=f32)
            grows[s, b] = big[:, :width]
            pre[...] = big[:, width:]

            def slopes(q, carry):
                at = pl.ds(pl.multiple_of(q * chunk, chunk), chunk)
                act[at, :] = (pre[at, :] * slope[s, b, at, :]).astype(bf16)
                return carry

            lax.fori_loop(0, nchunk, slopes, 0, unroll=2)
            acc[:, b * width : (b + 1) * width] = lax.dot_general(
                act[...], win_ref[...], NT, preferred_element_type=f32
            )
            for r in range(half):
                at = slice(r * tile, (r + 1) * tile)
                g = acc[at, b * width : (b + 1) * width] * gain_ref[...]
                z = normed[s, b, at, :]
                g = invs[s, b, at, :] * (
                    g
                    - jnp.mean(g, axis=1, keepdims=True)
                    - z * jnp.mean(g * z, axis=1, keepdims=True)
                )
                pad[s, rim + 2 * r + b, LEFT : LEFT + tile, :] = g
        strips(s, eg)
        for side in range(2):
            gz_copy(s, side).start()
        return carry

    lax.fori_loop(0, slots, backward, 0)
    vertical()
    for s in range(slots):
        for side in range(2):
            gz_copy(s, side).wait()
    lateral(hg)

    def last(s, carry):
        conv(s, True)
        for b in range(2):
            v = acc[:, (1 - b) * width : (2 - b) * width]
            v = mcol[s, b] * (grows[s, b] + v)
            out_ref[s, :, b] = v.reshape(half, tile, width).astype(bf16)
        return carry

    lax.fori_loop(0, slots, last, 0)


def on_device(
    inputs,
    slot_rows,
    cell_mask,
    target,
    dw_kernel,
    dw_bias,
    ln_gain,
    ln_bias,
    w_in,
    b_in,
    w_out,
    b_out,
    layer_scale,
    w_head,
):
    columns = lax.axis_size("tiles")
    members = lax.axis_size("ens")
    column = lax.axis_index("tiles")
    member = lax.axis_index("ens")
    slots, tile, _, width = inputs.shape[3:]
    size = dw_kernel.shape[0]
    rim = size // 2
    half = tile // 2
    nrow = half * tile
    hidden = w_in.shape[1]
    nv = w_head.shape[1]
    own_rows = lax.dynamic_index_in_dim(slot_rows, column, 0, keepdims=False)
    mask = (cell_mask[0, 0] * (own_rows >= 0)[:, None, None].astype(jnp.int32)).astype(bf16)
    m8 = mask.reshape(slots, half, 2, tile).transpose(0, 2, 1, 3).reshape(slots, 2, 1, nrow)
    m8 = jnp.broadcast_to(m8, (slots, 2, nv, nrow)).reshape(slots, 2 * nv, nrow)
    t8 = target[0, 0].reshape(slots, nv, half, 2, tile).transpose(0, 3, 1, 2, 4)
    t8 = t8.reshape(slots, 2 * nv, nrow)
    wh8 = jnp.concatenate([w_head.T, w_head.T], axis=0)
    vmem = pl.BlockSpec(memory_space=pltpu.VMEM)
    smem = pl.BlockSpec(memory_space=pltpu.SMEM)
    pairs = (tile + 2 * rim) // 2
    depth = (size + 1) // 2
    strip = (2, slots, rim, tile, width)
    halo = (2, slots + 1, rim, tile, width)
    dma = pltpu.SemaphoreType.DMA
    grad, score = pl.pallas_call(
        functools.partial(kernel, members, columns, slots=slots, tile=tile, size=size),
        out_shape=(
            jax.ShapeDtypeStruct((slots, half, 2, tile, width), bf16),
            jax.ShapeDtypeStruct((slots, 2, nrow), f32),
        ),
        in_specs=[smem] + [vmem] * 13,
        out_specs=(vmem, vmem),
        scratch_shapes=[
            pltpu.VMEM((slots, tile + 2 * rim, tile + 16, width), f32),
            pltpu.VMEM((size, pairs, tile, 2 * width), bf16),
            pltpu.VMEM((size, 2 * depth * width, 2 * width), bf16),
            pltpu.VMEM((nrow, 2 * width), f32),
            pltpu.VMEM((slots, 2, nrow, width), f32),
            pltpu.VMEM((slots, 2, nrow, width), f32),
            pltpu.VMEM((slots, 2, nrow, width), f32),
            pltpu.VMEM((slots, 2, nrow, width), f32),
            pltpu.VMEM((slots, 2, nrow, width), bf16),
            pltpu.VMEM((2, nrow, width), bf16),
            pltpu.VMEM((nrow, hidden), f32),
            pltpu.VMEM((nrow, hidden), bf16),
            pltpu.VMEM((slots, 2, nrow, hidden), f32),
            pltpu.VMEM(strip, bf16),
            pltpu.VMEM(halo, bf16),
            pltpu.VMEM(strip, bf16),
            pltpu.VMEM(halo, bf16),
            pltpu.VMEM((slots, 2 * nv, nrow), f32),
            pltpu.VMEM((members - 1, slots, 2 * nv, nrow), f32),
            dma((2,)),
            dma((2,)),
            dma((2, slots)),
            dma((2, slots)),
            dma((members - 1, slots)),
            dma((members - 1, slots)),
        ],
        compiler_params=pltpu.CompilerParams(
            collective_id=0, has_side_effects=True, vmem_limit_bytes=60 * 2**20
        ),
    )(
        slot_rows,
        inputs.reshape(slots, half, 2, tile, width),
        m8,
        t8,
        dw_kernel.transpose(1, 0, 2),
        dw_bias[None],
        ln_gain[None],
        ln_bias[None],
        w_in,
        b_in[None],
        w_out,
        b_out[None],
        layer_scale[None],
        wh8,
    )
    share = half // members
    score = score.reshape(slots, 2, half, tile)
    score = lax.dynamic_slice_in_dim(score, member * share, share, 2)
    score = score.transpose(0, 2, 1, 3).reshape(slots, 2 * share, tile).astype(bf16)
    return (grad.reshape(inputs.shape), score[None, None])


def solution(mesh):
    placed = (
        P("ens", "lev", ("groups", "tiles"), None, None, None, None),
        P("groups", None),
        P("lev", ("groups", "tiles"), None, None, None),
        P("lev", ("groups", "tiles"), None, None, None, None),
    ) + (P(),) * 10
    return jax.shard_map(
        on_device,
        mesh=mesh,
        in_specs=placed,
        out_specs=(
            P("ens", "lev", ("groups", "tiles"), None, None, None, None),
            P("lev", ("groups", "tiles"), None, "ens", None),
        ),
        check_vma=False,
    )
```

```python
import functools

import jax
import jax.numpy as jnp
from jax import lax
from jax.experimental import pallas as pl
from jax.experimental.pallas import tpu as pltpu
from jax.sharding import PartitionSpec as P

softness = 0.0625
epsilon = 1e-06
MESH = pl.DeviceIdType.MESH
f32 = jnp.float32
bf16 = jnp.bfloat16
LEFT = 8
NT = (((1,), (1,)), ((), ()))
TN = (((0,), (0,)), ((), ()))


def soft_abs(value):
    return jnp.sqrt(value * value + softness)


def soft_sign(value):
    return value * lax.rsqrt(value * value + softness)


def kernel(
    members,
    columns,
    rows_ref,
    x_ref,
    prep_ref,
    dw_ref,
    dwb_ref,
    gain_ref,
    lnb_ref,
    win_ref,
    bin_ref,
    wout_ref,
    bout_ref,
    ls_ref,
    wh8_ref,
    out_ref,
    crps_ref,
    pad,
    lhs,
    band,
    acc,
    normed,
    invs,
    grows,
    mcol,
    xm,
    feat,
    pre,
    act,
    slope,
    ex,
    hx,
    eg,
    hg,
    pmine,
    pall,
    sx,
    rx,
    sg,
    rg,
    sp,
    rp,
    *,
    slots,
    tile,
    size,
):
    rim = size // 2
    half = tile // 2
    width = x_ref.shape[-1]
    nrow = half * tile
    hidden = win_ref.shape[1]
    pairs = (tile + 2 * rim) // 2
    depth = (size + 1) // 2
    me = lax.axis_index("tiles")
    mine = lax.axis_index("ens")
    west = lax.rem(me + columns - 1, columns)
    east = lax.rem(me + 1, columns)

    barrier = pltpu.get_barrier_semaphore()
    pl.semaphore_signal(barrier, inc=1, device_id={"tiles": west}, device_id_type=MESH)
    pl.semaphore_signal(barrier, inc=1, device_id={"tiles": east}, device_id_type=MESH)
    for p in range(1, members):
        pl.semaphore_signal(
            barrier, inc=1, device_id={"ens": lax.rem(mine + p, members)}, device_id_type=MESH
        )

    sub8 = lax.broadcasted_iota(jnp.int32, (8, 1), 0)
    zero_strip = jnp.zeros((size // 2, tile, width), bf16)
    for side in range(2):
        hx[side, slots] = zero_strip
        hg[side, slots] = zero_strip

    def mask_rows(s):
        return jnp.where(
            sub8 < 4, prep_ref[s, 8:9].astype(f32), prep_ref[s, 9:10].astype(f32)
        )

    def mask_slot(s, carry):
        m8 = mask_rows(s).astype(bf16)
        for b in range(2):
            pick = jnp.broadcast_to((sub8 == 4 * b).astype(bf16), (8, width))
            col = lax.dot_general(m8, pick, TN, preferred_element_type=f32)
            mcol[s, b] = col
            xv = x_ref[s, :, b].astype(f32).reshape(nrow, width) * col
            xm[s, b] = xv.astype(bf16)
            x3 = xv.reshape(half, tile, width)
            for r in range(half):
                pad[s, rim + 2 * r + b, LEFT : LEFT + tile, :] = x3[r]
        return carry

    def strips(s, dst):
        for c in range(rim):
            dst[0, s, c] = pad[s, rim : rim + tile, LEFT + tile - rim + c, :].astype(bf16)
            dst[1, s, c] = pad[s, rim : rim + tile, LEFT + c, :].astype(bf16)

    lax.fori_loop(0, slots, mask_slot, 0)
    for s in range(slots):
        strips(s, ex)

    pl.semaphore_wait(barrier, 2 + members - 1)

    def edge_copy(src, dst, send, recv, side):
        return pltpu.make_async_remote_copy(
            src_ref=src,
            dst_ref=dst,
            send_sem=send,
            recv_sem=recv,
            device_id={"tiles": east if side == 0 else west},
            device_id_type=MESH,
        )

    x_copies = [
        edge_copy(ex.at[side], hx.at[side, pl.ds(0, slots)], sx.at[side], rx.at[side], side)
        for side in range(2)
    ]
    for copy in x_copies:
        copy.start()

    eye = lax.broadcasted_iota(jnp.int32, (width, width), 0) == lax.broadcasted_iota(
        jnp.int32, (width, width), 1
    )
    zero_block = jnp.zeros((width, width), bf16)

    def build_band(j, carry):
        for o in range(2 * depth):
            for b in range(2):
                i = o - b
                if 0 <= i < size:
                    row = dw_ref[i, pl.ds(j, 1), :]
                    block = jnp.where(eye, jnp.broadcast_to(row, (width, width)), 0.0).astype(bf16)
                else:
                    block = zero_block
                band[j, b, o * width : (o + 1) * width, :] = block
        return carry

    lax.fori_loop(0, size, build_band, 0)

    wh8 = wh8_ref[...]
    scaled_head = wh8 * ls_ref[...]
    through_head = lax.dot_general(
        scaled_head, wout_ref[...].astype(f32), NT, precision=lax.Precision.HIGHEST,
        preferred_element_type=f32,
    )
    bias_head = jnp.sum(scaled_head * bout_ref[...], axis=1, keepdims=True)
    both = jnp.concatenate([wh8, through_head], axis=1)
    both_hi = both.astype(bf16)
    both_lo = (both - both_hi.astype(f32)).astype(bf16)
    both_hl = jnp.concatenate([both_hi.astype(f32), both_lo.astype(f32)], axis=0).astype(bf16)
    sub16 = lax.broadcasted_iota(jnp.int32, (16, 1), 0)

    own = [rows_ref[me, s] for s in range(slots)]
    wrow = [rows_ref[west, s] for s in range(slots)]
    erow = [rows_ref[east, s] for s in range(slots)]

    def find(source, wanted):
        place = jnp.int32(slots)
        for t in range(slots):
            place = jnp.where((source[t] >= 0) & (source[t] == wanted), jnp.int32(t), place)
        return place

    def vertical():
        edge = jnp.zeros((rim, tile, width), f32)
        for s in range(slots):
            if s > 0:
                flag = ((own[s] >= 0) & (own[s - 1] == own[s] - 1)).astype(f32)
                pad[s, 0:rim, LEFT : LEFT + tile, :] = (
                    pad[s - 1, tile : tile + rim, LEFT : LEFT + tile, :] * flag
                )
            else:
                pad[s, 0:rim, LEFT : LEFT + tile, :] = edge
            if s < slots - 1:
                flag = ((own[s + 1] >= 0) & (own[s + 1] == own[s] + 1)).astype(f32)
                pad[s, tile + rim : tile + 2 * rim, LEFT : LEFT + tile, :] = (
                    pad[s + 1, rim : 2 * rim, LEFT : LEFT + tile, :] * flag
                )
            else:
                pad[s, tile + rim : tile + 2 * rim, LEFT : LEFT + tile, :] = edge

    def lateral(buf):
        for s in range(slots):
            for side, source in ((0, wrow), (1, erow)):
                up = find(source, own[s] - 1)
                level = find(source, own[s])
                down = find(source, own[s] + 1)
                for c in range(rim):
                    at = LEFT - rim + c if side == 0 else LEFT + tile + c
                    pad[s, rim : rim + tile, at, :] = buf[side, level, c].astype(f32)
                    pad[s, 0:rim, at, :] = buf[side, up, c].astype(f32)[tile - rim :]
                    pad[s, tile + rim : tile + 2 * rim, at, :] = buf[side, down, c].astype(f32)[
                        :rim
                    ]

    def product(s, j, flip):
        for a in range(2):
            for m in range(pairs):
                lhs[j, a, m] = pad[
                    s, 2 * m + a, LEFT - rim + j : LEFT - rim + j + tile, :
                ].astype(bf16)
        parts = []
        for d in range(depth):
            for a in range(2):
                at = depth - 1 - d if flip else d
                part = lhs[j, 1 - a if flip else a, at : at + half]
                parts.append(part.reshape(nrow, width))
        k = size - 1 - j if flip else j
        return jnp.dot(
            jnp.concatenate(parts, axis=1),
            jnp.concatenate([band[k, 0], band[k, 1]], axis=1),
            preferred_element_type=f32,
        )

    def centre(flip):
        def one(s, carry):
            acc[s] = product(s, rim, flip)
            return carry

        lax.fori_loop(0, slots, one, 0)

    def conv(s, flip):
        for j in range(size):
            if j != rim:
                acc[s] += product(s, j, flip)

    vertical()
    centre(False)
    for copy in x_copies:
        copy.wait()
    lateral(hx)

    chunk = 64
    nchunk = nrow // chunk

    def pred_copy(s, p):
        return pltpu.make_async_remote_copy(
            src_ref=pmine.at[s],
            dst_ref=pall.at[p - 1, s],
            send_sem=sp.at[p - 1, s],
            recv_sem=rp.at[p - 1, s],
            device_id={"ens": lax.rem(mine + p, members)},
            device_id_type=MESH,
        )

    def forward(s, carry):
        conv(s, False)
        for b in range(2):

            def norm(q, carry):
                at = pl.ds(pl.multiple_of(q * chunk, chunk), chunk)
                z = acc[s, at, b * width : (b + 1) * width] + dwb_ref[...]
                mean = jnp.mean(z, axis=1, keepdims=True)
                z = z - mean
                inv = lax.rsqrt(jnp.mean(z * z, axis=1, keepdims=True) + epsilon)
                z = z * inv
                normed[s, b, at, :] = z
                invs[s, b, at, :] = jnp.broadcast_to(inv, (chunk, width))
                feat[b, at, :] = (z * gain_ref[...] + lnb_ref[...]).astype(bf16)
                return carry

            lax.fori_loop(0, nchunk, norm, 0, unroll=2)
        res = []
        for b in range(2):
            pre[...] = jnp.dot(feat[b], win_ref[...], preferred_element_type=f32)

            def gelu(q, carry):
                at = pl.ds(pl.multiple_of(q * chunk, chunk), chunk)
                v = pre[at, :] + bin_ref[...]
                cum = 0.5 * (1.0 + lax.erf(v * 0.7071067811865476))
                act[at, :] = (v * cum).astype(bf16)
                slope[s, b, at, :] = cum + v * jnp.exp(-0.5 * v * v) * 0.3989422804014327
                return carry

            lax.fori_loop(0, nchunk, gelu, 0, unroll=2)
            r16 = lax.dot_general(
                both_hl,
                jnp.concatenate([xm[s, b], act[...]], axis=1),
                NT,
                preferred_element_type=f32,
            )
            res.append(r16[:8] + r16[8:])
        pmine[s] = jnp.where(sub8 < 4, res[0], res[1]) + bias_head
        for p in range(1, members):
            pred_copy(s, p).start()
        return carry

    lax.fori_loop(0, slots, forward, 0)

    def gz_copy(s, side):
        return edge_copy(eg.at[side, s], hg.at[side, s], sg.at[side, s], rg.at[side, s], side)

    def backward(s, carry):
        for p in range(1, members):
            pred_copy(s, p).wait()
        every = [pmine[s]] + [pall[p - 1, s] for p in range(1, members)]
        goal = prep_ref[s, 0:8].astype(f32)
        mask = mask_rows(s)
        skill = soft_abs(every[0] - goal)
        spread = jnp.zeros_like(skill)
        pull = jnp.zeros_like(skill)
        for p in range(1, members):
            skill = skill + soft_abs(every[p] - goal)
            pull = pull + soft_sign(every[0] - every[p])
            for other in range(p):
                spread = spread + soft_abs(every[p] - every[other])
        diagonal = members * softness**0.5
        score = mask * (
            skill / members - (2.0 * spread + diagonal) / (2 * members * members)
        )
        share = half // members
        for b in range(2):
            total = jnp.sum(score[4 * b : 4 * b + 4], axis=0, keepdims=True)
            for r in range(share):
                piece = total[:, r * tile : (r + 1) * tile]
                for p in range(1, members):
                    at = (p * share + r) * tile
                    piece = jnp.where(mine == p, total[:, at : at + tile], piece)
                crps_ref[s, 2 * r + b : 2 * r + b + 1, :] = piece
        gp = mask * (soft_sign(every[0] - goal) / members - pull / (members * members))
        gp = gp.astype(bf16).astype(f32)
        gp16 = jnp.concatenate([gp, gp], axis=0).astype(bf16)
        for b in range(2):
            rows = (lax.rem(sub16, 8) // 4) == b
            wb = jnp.where(rows, both_hl.astype(f32), 0.0).astype(bf16)
            big = lax.dot_general(gp16, wb, TN, preferred_element_type=f32)
            grows[s, b] = big[:, :width]
            pre[...] = big[:, width:]

            def slopes(q, carry):
                at = pl.ds(pl.multiple_of(q * chunk, chunk), chunk)
                act[at, :] = (pre[at, :] * slope[s, b, at, :]).astype(bf16)
                return carry

            lax.fori_loop(0, nchunk, slopes, 0, unroll=2)
            acc[s, :, b * width : (b + 1) * width] = lax.dot_general(
                act[...], win_ref[...], NT, preferred_element_type=f32
            )
            for r in range(half):
                at = slice(r * tile, (r + 1) * tile)
                g = acc[s, at, b * width : (b + 1) * width] * gain_ref[...]
                z = normed[s, b, at, :]
                g = invs[s, b, at, :] * (
                    g
                    - jnp.mean(g, axis=1, keepdims=True)
                    - z * jnp.mean(g * z, axis=1, keepdims=True)
                )
                pad[s, rim + 2 * r + b, LEFT : LEFT + tile, :] = g
        strips(s, eg)
        for side in range(2):
            gz_copy(s, side).start()
        return carry

    lax.fori_loop(0, slots, backward, 0)
    vertical()
    centre(True)
    for s in range(slots):
        for side in range(2):
            gz_copy(s, side).wait()
    lateral(hg)

    def last(s, carry):
        conv(s, True)
        for b in range(2):
            v = acc[s, :, (1 - b) * width : (2 - b) * width]
            v = mcol[s, b] * (grows[s, b] + v)
            out_ref[s, :, b] = v.reshape(half, tile, width).astype(bf16)
        return carry

    lax.fori_loop(0, slots, last, 0)


def on_device(
    inputs,
    slot_rows,
    cell_mask,
    target,
    dw_kernel,
    dw_bias,
    ln_gain,
    ln_bias,
    w_in,
    b_in,
    w_out,
    b_out,
    layer_scale,
    w_head,
):
    columns = lax.axis_size("tiles")
    members = lax.axis_size("ens")
    column = lax.axis_index("tiles")
    slots, tile, _, width = inputs.shape[3:]
    size = dw_kernel.shape[0]
    rim = size // 2
    half = tile // 2
    nrow = half * tile
    hidden = w_in.shape[1]
    nv = w_head.shape[1]
    own_rows = lax.dynamic_index_in_dim(slot_rows, column, 0, keepdims=False)
    mask = (cell_mask[0, 0] * (own_rows >= 0)[:, None, None].astype(jnp.int32)).astype(bf16)
    m2 = mask.reshape(slots, half, 2, tile).transpose(0, 2, 1, 3)
    t8 = target[0, 0].reshape(slots, nv, half, 2, tile).transpose(0, 3, 1, 2, 4)
    t8 = t8.reshape(slots, 2 * nv, half, tile)
    prep = jnp.concatenate([t8, m2], axis=1).reshape(slots, 2 * nv + 2, nrow)
    wh8 = jnp.concatenate([w_head.T, w_head.T], axis=0)
    vmem = pl.BlockSpec(memory_space=pltpu.VMEM)
    smem = pl.BlockSpec(memory_space=pltpu.SMEM)
    pairs = (tile + 2 * rim) // 2
    depth = (size + 1) // 2
    strip = (2, slots, rim, tile, width)
    halo = (2, slots + 1, rim, tile, width)
    dma = pltpu.SemaphoreType.DMA
    grad, score = pl.pallas_call(
        functools.partial(kernel, members, columns, slots=slots, tile=tile, size=size),
        out_shape=(
            jax.ShapeDtypeStruct((slots, half, 2, tile, width), bf16),
            jax.ShapeDtypeStruct((slots, tile // members, tile), f32),
        ),
        in_specs=[smem] + [vmem] * 12,
        out_specs=(vmem, vmem),
        scratch_shapes=[
            pltpu.VMEM((slots, tile + 2 * rim, tile + 16, width), f32),
            pltpu.VMEM((size, 2, pairs, tile, width), bf16),
            pltpu.VMEM((size, 2, 2 * depth * width, width), bf16),
            pltpu.VMEM((slots, nrow, 2 * width), f32),
            pltpu.VMEM((slots, 2, nrow, width), f32),
            pltpu.VMEM((slots, 2, nrow, width), f32),
            pltpu.VMEM((slots, 2, nrow, width), f32),
            pltpu.VMEM((slots, 2, nrow, width), f32),
            pltpu.VMEM((slots, 2, nrow, width), bf16),
            pltpu.VMEM((2, nrow, width), bf16),
            pltpu.VMEM((nrow, hidden), f32),
            pltpu.VMEM((nrow, hidden), bf16),
            pltpu.VMEM((slots, 2, nrow, hidden), f32),
            pltpu.VMEM(strip, bf16),
            pltpu.VMEM(halo, bf16),
            pltpu.VMEM(strip, bf16),
            pltpu.VMEM(halo, bf16),
            pltpu.VMEM((slots, 2 * nv, nrow), f32),
            pltpu.VMEM((members - 1, slots, 2 * nv, nrow), f32),
            dma((2,)),
            dma((2,)),
            dma((2, slots)),
            dma((2, slots)),
            dma((members - 1, slots)),
            dma((members - 1, slots)),
        ],
        compiler_params=pltpu.CompilerParams(
            collective_id=0, has_side_effects=True, vmem_limit_bytes=60 * 2**20
        ),
    )(
        slot_rows,
        inputs.reshape(slots, half, 2, tile, width),
        prep,
        dw_kernel,
        dw_bias[None],
        ln_gain[None],
        ln_bias[None],
        w_in,
        b_in[None],
        w_out,
        b_out[None],
        layer_scale[None],
        wh8,
    )
    return (grad.reshape(inputs.shape), score.astype(bf16)[None, None])


def solution(mesh):
    placed = (
        P("ens", "lev", ("groups", "tiles"), None, None, None, None),
        P("groups", None),
        P("lev", ("groups", "tiles"), None, None, None),
        P("lev", ("groups", "tiles"), None, None, None, None),
    ) + (P(),) * 10
    return jax.shard_map(
        on_device,
        mesh=mesh,
        in_specs=placed,
        out_specs=(
            P("ens", "lev", ("groups", "tiles"), None, None, None, None),
            P("lev", ("groups", "tiles"), None, "ens", None),
        ),
        check_vma=False,
    )
```
